32 devices in a mesh: samp: 4 (over y, core), snp: 8 (over z, x).
Axes of the slice: x: 2, y: 2, z: 4, core: 2. Of those that a mesh axis runs over, the one named last changes fastest.
Arguments:
- dosage: int32 [384, 2048], P('snp', 'samp'), may hold values from 0 to 2
- pheno: bfloat16 [2048, 2048], P('samp'), may hold values from -6 to 6
- perm: int32 [8, 2048], P(None, 'samp'), may hold values from 0 to 2047, each once within a row
- snp_weight: float32 [384], P('snp'), may hold values from 0.015 to 64
Outputs:
- whitened: bfloat16 [9, 384, 2048], P(None, 'snp', 'samp')
The draws below stay inside these ranges and needn't reach their ends.
Inputs may be any that keep to these rules, and one draw needn't show every extreme that they name: `perm`: each of the 8 rows names every sample index exactly once.
All inputs are finite; a program needn't handle non-finite values.
Results may differ from the reference program's by a relative error of at most 0.012.
Values may be sent and summed in bfloat16 or wider, within the bound.
No kernel may reach another device: no remote copies, remote signals or barrier semaphores. Data moves between devices by JAX's collectives and lax.ppermute only.
A program may use at most 64 MiB of HBM per device.

```python
import jax
import jax.numpy as jnp
from jax import lax

G = 2048
NULLS = 8
SNP_DEV = 48
COPIES = 9
NS = 2048
NSNP = 384


def draw_snp_weight(key, part):
    slabs = NSNP // SNP_DEV
    slab_draw = jax.random.uniform(jax.random.fold_in(key, 11), (slabs,), jnp.float32)
    snp_draw = jax.random.uniform(jax.random.fold_in(key, 12), (NSNP,), jnp.float32)
    exponent = jnp.repeat(2.0 * slab_draw - 1.0, SNP_DEV) + 0.2 * (2.0 * snp_draw - 1.0)
    return jnp.power(10.0, exponent).astype(jnp.float32)


def draw_pheno(key, part):
    values = jax.random.normal(jax.random.fold_in(key, 24), (NS, G), jnp.float32)
    return jnp.clip(values, -6.0, 6.0).astype(jnp.bfloat16)


def place_ends(values, stream_key, low, largest):
    shape = values.shape
    index_at = [jax.random.randint(jax.random.fold_in(stream_key, axis), (), 0, shape[axis]) for axis in range(len(shape))]
    values = values.at[tuple(index_at)].set(low)
    longest = shape.index(max(shape))
    index_at[longest] = (index_at[longest] + 1) % shape[longest]
    return values.at[tuple(index_at)].set(largest)


def setup_inputs(seed: int = 0) -> dict:
    seeds = jax.random.split(jax.random.key(seed), 5)
    dosage = place_ends(jax.random.randint(seeds[0], (NSNP, NS), 0, 3), jax.random.fold_in(seeds[0], 1), 0, 2).astype(jnp.int32)
    pheno = draw_pheno(jax.random.fold_in(seeds[4], 71), 0)
    perm = jax.vmap(lambda own: jax.random.permutation(own, NS))(jax.random.split(seeds[2], NULLS)).reshape((NULLS, NS)).astype(jnp.int32)
    snp_weight = draw_snp_weight(jax.random.fold_in(seeds[4], 71), 0)
    return dict(dosage=dosage, pheno=pheno, perm=perm, snp_weight=snp_weight)


def reference(dosage, pheno, perm, snp_weight):
    dose = dosage.astype(jnp.float32)
    dose_mean = lax.optimization_barrier(jnp.mean(dose, axis=1))
    dose_square = lax.optimization_barrier(jnp.mean(dose * dose, axis=1))
    pheno_total = lax.optimization_barrier(jnp.sum(pheno.astype(jnp.float32), axis=0))
    dose_half = dosage.astype(jnp.bfloat16)
    own_rows = jnp.arange(NS).astype(jnp.int32)
    sources = jnp.concatenate([own_rows[None, :], perm.astype(jnp.int32)], axis=0)

    def one_copy(source):
        return jnp.dot(dose_half, pheno[source], preferred_element_type=jnp.float32)
    raw_scores = lax.map(one_copy, sources)
    spread = jnp.sqrt(NS * (dose_square + 1e-05))
    scores = ((raw_scores - dose_mean[None, :, None] * pheno_total[None, None, :]) / spread[None, :, None]).astype(jnp.bfloat16)
    flat = scores.reshape(COPIES * NSNP, G)
    null_scores = flat[NSNP:]
    weight_rows = jnp.tile(snp_weight.astype(jnp.float32), NULLS)[:, None]
    weighted = (null_scores.astype(jnp.float32) * weight_rows).astype(jnp.bfloat16)
    gram = lax.dot_general(weighted, null_scores, (((0,), (0,)), ((), ())), preferred_element_type=jnp.float32) / (NULLS * NSNP)
    scale = jnp.trace(gram) / G + 1e-06
    scaled = gram / scale
    identity = jnp.eye(G, dtype=jnp.float32)
    first_step = ((3.0 * identity - scaled) * 0.5).astype(jnp.bfloat16)
    first_image = jnp.dot(scaled.astype(jnp.bfloat16), first_step, preferred_element_type=jnp.float32).astype(jnp.bfloat16)
    second_prod = jnp.dot(first_step, first_image, preferred_element_type=jnp.float32)
    second_step = ((3.0 * identity - second_prod) * 0.5).astype(jnp.bfloat16)
    root_approx = jnp.dot(second_step, first_step, preferred_element_type=jnp.float32)
    root_matrix = (root_approx / jnp.sqrt(scale)).astype(jnp.bfloat16)
    white = jnp.dot(flat, root_matrix, preferred_element_type=jnp.float32)
    return white.astype(jnp.bfloat16).reshape(COPIES, NSNP, G)
```

```python
import functools

import jax
import jax.numpy as jnp
from jax import lax
from jax.experimental import pallas as pl
from jax.experimental.pallas import tpu as pltpu
from jax.sharding import PartitionSpec as P

LANES = 128
PACK = 3
BLOCKS = 8
REACH = 5
AXES = ("samp", "snp")


ANY = pl.BlockSpec(memory_space=pl.ANY)
VMEM = pl.BlockSpec(memory_space=pltpu.VMEM)
BF16 = jnp.bfloat16
F32 = jnp.float32


def permute(value, samp_count, snp_count, move):
    pairs = []
    for samp in range(samp_count):
        for snp in range(snp_count):
            samp_to, snp_to = move(samp, snp)
            pairs.append((samp * snp_count + snp, samp_to * snp_count + snp_to))
    return lax.ppermute(value, AXES, pairs)


def score_kernel(copies, snp_rows, block, half, total_samples, *refs):
    smalls = refs[0:4]
    pheno_ref, mate_ref, total_ref = refs[4:7]
    chunk_refs = refs[7:11]
    first_ref = refs[11]
    picked, genes, sems = refs[12:15]
    samp = lax.axis_index("samp")
    core = lax.rem(samp, 2)
    mate = samp + 1 - 2 * core
    own_cols = pl.ds(pl.multiple_of(core * half, half), half)
    fetch_own = pltpu.make_async_copy(
        pheno_ref.at[:, own_cols], genes.at[pl.ds(0, block), :], sems.at[0]
    )
    fetch_mate = pltpu.make_async_copy(mate_ref, genes.at[pl.ds(block, block), :], sems.at[1])
    fetch_own.start()
    fetch_mate.start()
    nulls = copies - 1
    loaded = [small[...].astype(jnp.int32) for small in smalls]
    dose = [value[:snp_rows] for value in loaded]
    perm = jnp.concatenate([value[snp_rows:] for value in loaded], axis=1)
    dose_all = jnp.concatenate(dose, axis=1)
    rows = snp_rows // PACK
    packed = dose_all[:rows]
    for part in range(1, PACK):
        packed = packed + dose_all[part * rows : (part + 1) * rows] * (4**part)
    packed = packed.astype(F32).astype(BF16)
    dose_float = dose_all.astype(F32)
    dose_mean = jnp.sum(dose_float, axis=1, keepdims=True) / total_samples
    dose_square = jnp.sum(dose_float * dose_float, axis=1, keepdims=True) / total_samples
    inv_spread = lax.rsqrt(total_samples * (dose_square + 1e-05))
    groups = block // LANES
    high = (perm // LANES).astype(F32).astype(BF16)
    low = (perm % LANES).astype(F32).astype(BF16)
    lane_ids = lax.broadcasted_iota(jnp.int32, (LANES, dose_all.shape[1]), 0)
    lane_ids = lane_ids.astype(F32).astype(BF16)
    one = jnp.ones((), BF16)
    zero = jnp.zeros((), BF16)
    group_ids = [samp * groups + group for group in range(groups)]
    group_ids += [mate * groups + group for group in range(groups)]
    group_ids = [value.astype(F32).astype(BF16) for value in group_ids]
    for copy in range(nulls):
        onehot = jnp.where(lane_ids == low[copy : copy + 1], one, zero)
        masked = jnp.concatenate(
            [jnp.where(high[copy : copy + 1] == value, packed, zero) for value in group_ids],
            axis=0,
        )
        spots = lax.dot_general(
            masked, onehot, (((1,), (1,)), ((), ())), preferred_element_type=F32
        ).astype(jnp.int32)
        for group in range(2 * groups):
            piece = spots[group * rows : (group + 1) * rows]
            for part in range(PACK):
                at = (copy + 1) * snp_rows + part * rows
                picked[at : at + rows, group * LANES : (group + 1) * LANES] = (
                    lax.shift_right_logical(piece, 2 * part) & 3
                ).astype(F32).astype(BF16)
    picked[:snp_rows, :block] = dose[0].astype(F32).astype(BF16)
    picked[:snp_rows, block:] = dose[1].astype(F32).astype(BF16)
    all_rows = copies * snp_rows
    picked[all_rows:, :] = jnp.ones((picked.shape[0] - all_rows, 2 * block), BF16)
    row_sum = jnp.sum(picked[:all_rows].astype(F32), axis=1, keepdims=True)
    mean_rows = jnp.concatenate([dose_mean] * copies, axis=0)
    inv_rows = jnp.concatenate([inv_spread] * copies, axis=0)
    excess = row_sum - mean_rows * (2.0 * block)
    fetch_own.wait()
    fetch_mate.wait()
    width = half // len(chunk_refs)
    for chunk in range(len(chunk_refs)):
        cols = slice(chunk * width, (chunk + 1) * width)
        raw = jnp.dot(picked[...], genes[:, cols], preferred_element_type=F32)
        at = pl.ds(pl.multiple_of(core * half + chunk * width, width), width)
        center = total_ref[:, at] / total_samples
        part = (
            raw[:all_rows] - mean_rows * raw[all_rows : all_rows + 1] - center * excess
        ) * inv_rows
        part = part.astype(BF16)
        chunk_refs[chunk][...] = part[snp_rows:]
        first_ref[:, cols] = part[:snp_rows]


def gram_kernel(pieces, *refs):
    inputs = refs[0:16]
    weight_ref, mate_weight_ref = refs[16:18]
    outs = refs[18 : 18 + pieces]
    held, strip, sems = refs[18 + pieces :]
    rows = inputs[0].shape[0]
    width = inputs[0].shape[1]
    copies = []
    for slab in range(2):
        for place in range(8):
            copies.append(
                pltpu.make_async_copy(
                    inputs[slab * 8 + place],
                    held.at[pl.ds(slab * rows, rows), pl.ds(place * width, width)],
                    sems.at[slab * 8 + place],
                )
            )
            copies[-1].start()
    for copy in copies:
        copy.wait()
    samp = lax.axis_index("samp")
    snp = lax.axis_index("snp")
    first = (samp // 2) * 2 + lax.rem(snp, 2)
    depth = snp // 2
    own = held[:, pl.ds(pl.multiple_of(first * width, width), width)].astype(F32)
    scaled = jnp.concatenate(
        [own[:rows] * weight_ref[:, :1], own[rows:] * mate_weight_ref[:, :1]], axis=0
    ).astype(BF16)
    for reach in range(REACH):
        at = pl.ds(pl.multiple_of((first + reach) * width, width), width)
        strip[:, reach * width : (reach + 1) * width] = lax.dot_general(
            scaled, held[:, at], (((0,), (0,)), ((), ())), preferred_element_type=F32
        )
    size = width // pieces
    for step in range(pieces):
        at = lax.rem(depth + step, pieces) * size
        outs[step][...] = strip[pl.ds(pl.multiple_of(at, size), size), :].astype(BF16)


def chain_kernel(pieces, total_rows, *refs):
    strips = refs[0:16]
    nulls = refs[16:24]
    firsts = refs[24:26]
    out_ref = refs[26]
    matrix, kept, current, sems = refs[27:31]
    samp = lax.axis_index("samp")
    snp = lax.axis_index("snp")
    core = lax.rem(samp, 2)
    side = samp // 2
    minor = lax.rem(snp, 2)
    depth = snp // 2
    width = nulls[0].shape[1]
    genes = matrix.shape[0]
    size = width // pieces
    part_cols = strips[0].shape[1]
    null_rows = nulls[0].shape[0] // 2
    first_rows = kept.shape[0] - null_rows
    copies = []
    for core_flip in range(2):
        for side_flip in range(2):
            for minor_flip in range(2):
                block = (
                    (core + core_flip - 2 * core * core_flip) * 4
                    + (side + side_flip - 2 * side * side_flip) * 2
                    + (minor + minor_flip - 2 * minor * minor_flip)
                )
                for part in range(2):
                    source = strips[core_flip * 8 + side_flip * 4 + minor_flip * 2 + part]
                    cuts = sorted(
                        {part * part_cols, (part + 1) * part_cols}
                        | {
                            edge * width
                            for edge in range(REACH + 1)
                            if part * part_cols < edge * width < (part + 1) * part_cols
                        }
                    )
                    for low, high in zip(cuts[:-1], cuts[1:]):
                        reach = low // width
                        column = lax.rem(block + reach, BLOCKS) * width + (low - reach * width)
                        column = pl.multiple_of(column, LANES)
                        for step in range(pieces):
                            row = block * width + lax.rem(depth - step + pieces, pieces) * size
                            copies.append(
                                pltpu.make_async_copy(
                                    source.at[
                                        pl.ds(step * size, size),
                                        pl.ds(low - part * part_cols, high - low),
                                    ],
                                    matrix.at[
                                        pl.ds(pl.multiple_of(row, size), size),
                                        pl.ds(column, high - low),
                                    ],
                                    sems.at[0],
                                )
                            )
                            copies[-1].start()
    copies = []
    for flip in range(2):
        holder = core + flip - 2 * core * flip
        for chunk in range(4):
            column = pl.multiple_of((holder * 4 + chunk) * width, width)
            copies.append(
                pltpu.make_async_copy(
                    nulls[flip * 4 + chunk].at[
                        pl.ds(pl.multiple_of(core * null_rows, null_rows), null_rows), :
                    ],
                    kept.at[pl.ds(0, null_rows), pl.ds(column, width)],
                    sems.at[1],
                )
            )
            copies[-1].start()
        half = genes // 2
        skip = firsts[0].shape[0] - first_rows
        copies.append(
            pltpu.make_async_copy(
                firsts[flip].at[pl.ds(pl.multiple_of(core * skip, 16), first_rows), :],
                kept.at[
                    pl.ds(null_rows, first_rows), pl.ds(pl.multiple_of(holder * half, half), half)
                ],
                sems.at[1],
            )
        )
        copies[-1].start()
    filled = matrix.at[pl.ds(0, REACH * width), :]
    pltpu.make_async_copy(filled, filled, sems.at[0]).wait()
    pltpu.make_async_copy(kept, kept, sems.at[1]).wait()

    trace = jnp.zeros((1, 1), F32)
    eye = lax.broadcasted_iota(jnp.int32, (width, width), 0) == lax.broadcasted_iota(
        jnp.int32, (width, width), 1
    )
    for block in range(BLOCKS):
        at = slice(block * width, (block + 1) * width)
        values = jnp.where(eye, matrix[at, at].astype(F32), 0.0)
        trace = trace + jnp.sum(jnp.sum(values, axis=1, keepdims=True), axis=0, keepdims=True)
    scale = trace / total_rows / genes + 1e-06
    factor = 0.5 / (total_rows * scale)

    def mirror(block, carry):
        for reach in range(1, REACH - 1):
            source = pl.multiple_of(lax.rem(block + reach, BLOCKS) * width, width)
            target = pl.multiple_of(block * width, width)
            tile = matrix[pl.ds(target, width), pl.ds(source, width)]
            matrix[pl.ds(source, width), pl.ds(target, width)] = tile.T
        return carry

    lax.fori_loop(0, BLOCKS, mirror, 0)

    def apply(source, target):
        def one(block, carry):
            at = pl.ds(pl.multiple_of(block * width, width), width)
            image = jnp.dot(source[...], matrix[:, at], preferred_element_type=F32)
            target[:, at] = (1.5 * source[:, at].astype(F32) - factor * image).astype(BF16)
            return carry

        lax.fori_loop(0, BLOCKS, one, 0)

    first_image, second_image = current.at[0], current.at[1]
    apply(kept, first_image)
    apply(first_image, second_image)
    apply(second_image, kept)
    inverse = lax.rsqrt(scale)
    quarter = genes // 4
    for flip in range(2):
        holder = core + flip - 2 * core * flip
        base = side * (genes // 2) + holder * quarter
        for inner in range(quarter // width):
            at = pl.ds(pl.multiple_of(base + inner * width, width), width)
            image = jnp.dot(kept[...], matrix[:, at], preferred_element_type=F32)
            value = (1.5 * first_image[:, at].astype(F32) - factor * image) * inverse
            out_ref[flip, :, inner * width : (inner + 1) * width] = value.astype(BF16)


def shards(samp_count, snp_count, dosage, pheno, perm, snp_weight):
    snp_rows, block = dosage.shape
    genes = pheno.shape[1]
    total_samples = block * samp_count
    total_snps = snp_rows * snp_count
    null_count = perm.shape[0]
    copies = null_count + 1
    half = genes // 2
    width = genes // BLOCKS
    chunks = half // width
    null_rows = null_count * snp_rows
    pieces = snp_count // 2
    size = width // pieces
    move = functools.partial(permute, samp_count=samp_count, snp_count=snp_count)
    over_core = functools.partial(move, move=lambda a, b: (a ^ 1, b))
    over_side = functools.partial(move, move=lambda a, b: (a ^ 2, b))
    over_both = functools.partial(move, move=lambda a, b: (a ^ 3, b))
    over_minor = functools.partial(move, move=lambda a, b: (a, b ^ 1))

    def over_depth(value, step):
        return move(value, move=lambda a, b: (a, (b + 2 * step) % snp_count))

    core = lax.axis_index("samp") % 2
    small = jnp.concatenate([dosage, perm], axis=0).astype(jnp.int16)
    smalls = [small, over_core(small), over_side(small), over_both(small)]
    mate_cols = lax.dynamic_slice_in_dim(pheno, (1 - core) * half, half, 1)
    mate_rows = over_core(mate_cols)
    own_total = jnp.sum(pheno.astype(F32), axis=0, keepdims=True)
    total = (own_total + over_core(own_total)) + (over_side(own_total) + over_both(own_total))
    mate_weight = over_minor(snp_weight)
    weights = [
        jnp.broadcast_to(jnp.tile(value, null_count)[:, None], (null_rows, LANES))
        for value in (snp_weight, mate_weight)
    ]

    all_rows = copies * snp_rows
    parts = pl.pallas_call(
        functools.partial(score_kernel, copies, snp_rows, block, half, float(total_samples)),
        out_shape=[jax.ShapeDtypeStruct((null_rows, width), BF16)] * chunks
        + [jax.ShapeDtypeStruct((snp_rows, half), BF16)],
        in_specs=[VMEM] * 4 + [ANY, ANY, VMEM],
        out_specs=[VMEM] * (chunks + 1),
        scratch_shapes=[
            pltpu.VMEM((all_rows + 16, 2 * block), BF16),
            pltpu.VMEM((2 * block, half), BF16),
            pltpu.SemaphoreType.DMA((2,)),
        ],
        name="score",
    )(*smalls, pheno, mate_rows, total)

    def finish(value):
        return (value.astype(F32) + over_side(value).astype(F32)).astype(BF16)

    own = [finish(value) for value in parts[:chunks]]
    own_first = finish(parts[chunks])
    mate = [over_core(value) for value in own]
    minor = [over_minor(value) for value in own]
    minor_mate = [over_core(value) for value in minor]
    mate_first = over_core(own_first)

    strips = pl.pallas_call(
        functools.partial(gram_kernel, pieces),
        out_shape=[jax.ShapeDtypeStruct((size, REACH * width), BF16)] * pieces,
        in_specs=[ANY] * 16 + [VMEM] * 2,
        out_specs=[VMEM] * pieces,
        scratch_shapes=[
            pltpu.VMEM((2 * null_rows, genes), BF16),
            pltpu.VMEM((width, REACH * width), F32),
            pltpu.SemaphoreType.DMA((16,)),
        ],
        name="gram",
    )(*own, *mate, *minor, *minor_mate, *weights)

    piece = strips[0].astype(F32)
    for step in range(1, pieces):
        piece = piece + over_depth(strips[step], step).astype(F32)
    piece = piece.astype(BF16)
    part_cols = REACH * width // 2
    gathered = []
    for part in range(2):
        mine = piece[:, part * part_cols : (part + 1) * part_cols]
        gathered.append(
            jnp.concatenate(
                [mine] + [over_depth(mine, step) for step in range(1, pieces)], axis=0
            )
        )
    a_own, b_own = gathered
    a_side, b_minor = over_side(a_own), over_minor(b_own)
    a_minor, b_side = over_minor(a_own), over_side(b_own)
    a_far, b_far = over_minor(a_side), over_side(b_minor)
    quarter = [a_own, b_own, a_minor, b_minor, a_side, b_side, a_far, b_far]
    quarter_mate = [over_core(value) for value in quarter]

    first_rows = 32
    work_rows = null_rows // 2 + first_rows
    result = pl.pallas_call(
        functools.partial(chain_kernel, pieces, float(null_count * total_snps)),
        out_shape=jax.ShapeDtypeStruct((2, work_rows, genes // samp_count), BF16),
        in_specs=[ANY] * 26,
        out_specs=VMEM,
        scratch_shapes=[
            pltpu.VMEM((genes, genes), BF16),
            pltpu.VMEM((work_rows, genes), BF16),
            pltpu.VMEM((2, work_rows, genes), BF16),
            pltpu.SemaphoreType.DMA((2,)),
        ],
        name="chain",
    )(*quarter, *quarter_mate, *own, *mate, own_first, mate_first)

    mine = result[0]
    theirs = over_core(result[1])
    low = jnp.where(core == 0, mine, theirs)
    high = jnp.where(core == 0, theirs, mine)
    half_null = null_rows // 2
    spare = 2 * first_rows - snp_rows
    white = jnp.concatenate(
        [
            low[half_null:],
            high[half_null + spare :],
            low[:half_null],
            high[:half_null],
        ],
        axis=0,
    )
    return white.reshape(copies, snp_rows, genes // samp_count)


def solution(mesh):
    return jax.shard_map(
        functools.partial(shards, mesh.shape["samp"], mesh.shape["snp"]),
        mesh=mesh,
        in_specs=(P("snp", "samp"), P("samp", None), P(None, "samp"), P("snp")),
        out_specs=P(None, "snp", "samp"),
        check_vma=False,
    )
```

```python
import functools

import jax
import jax.numpy as jnp
from jax import lax
from jax.experimental import pallas as pl
from jax.experimental.pallas import tpu as pltpu
from jax.sharding import PartitionSpec as P

LANES = 128
PACK = 3
BLOCKS = 16
REACH = 9
CHUNK_LANES = (3, 2, 2, 1)
GROUPS = 4
AXES = ("samp", "snp")


ANY = pl.BlockSpec(memory_space=pl.ANY)
VMEM = pl.BlockSpec(memory_space=pltpu.VMEM)
BF16 = jnp.bfloat16
F32 = jnp.float32


def permute(value, samp_count, snp_count, move):
    pairs = []
    for samp in range(samp_count):
        for snp in range(snp_count):
            samp_to, snp_to = move(samp, snp)
            pairs.append((samp * snp_count + snp, samp_to * snp_count + snp_to))
    return lax.ppermute(value, AXES, pairs)


def flip_bit(value, flip):
    return value + flip - 2 * value * flip


def score_kernel(copies, snp_rows, block, half, total_samples, *refs):
    smalls = refs[0:4]
    pheno_ref, mate_ref, weight_ref = refs[4:7]
    chunk_refs = refs[7:11]
    first_ref, mean_ref, excess_ref, first_excess_ref, spread_weight_ref = refs[11:16]
    picked, genes, sems = refs[16:19]
    samp = lax.axis_index("samp")
    core = lax.rem(samp, 2)
    mate = flip_bit(core, 1) - core + samp
    own_cols = pl.ds(pl.multiple_of(core * half, half), half)
    fetches = [
        pltpu.make_async_copy(
            source.at[:, own_cols], genes.at[pl.ds(place * block, block), :], sems.at[place]
        )
        for place, source in enumerate((pheno_ref, mate_ref))
    ]
    for fetch in fetches:
        fetch.start()
    nulls = copies - 1
    loaded = [small[...].astype(jnp.int32) for small in smalls]
    dose = [value[:snp_rows] for value in loaded]
    perm = jnp.concatenate([value[snp_rows:] for value in loaded], axis=1)
    dose_all = jnp.concatenate(dose, axis=1)
    rows = snp_rows // PACK
    packed = dose_all[:rows]
    for part in range(1, PACK):
        packed = packed + dose_all[part * rows : (part + 1) * rows] * (4**part)
    packed = packed.astype(F32).astype(BF16)
    dose_float = dose_all.astype(F32)
    dose_mean = jnp.sum(dose_float, axis=1, keepdims=True) / total_samples
    dose_square = jnp.sum(dose_float * dose_float, axis=1, keepdims=True) / total_samples
    inv_spread = lax.rsqrt(total_samples * (dose_square + 1e-05))
    groups = block // LANES
    high = (perm // LANES).astype(F32).astype(BF16)
    low = (perm % LANES).astype(F32).astype(BF16)
    lane_ids = lax.broadcasted_iota(jnp.int32, (LANES, dose_all.shape[1]), 0)
    lane_ids = lane_ids.astype(F32).astype(BF16)
    one = jnp.ones((), BF16)
    zero = jnp.zeros((), BF16)
    group_ids = [samp * groups + group for group in range(groups)]
    group_ids += [mate * groups + group for group in range(groups)]
    group_ids = [value.astype(F32).astype(BF16) for value in group_ids]
    for copy in range(nulls):
        onehot = jnp.where(lane_ids == low[copy : copy + 1], one, zero)
        masked = jnp.concatenate(
            [jnp.where(high[copy : copy + 1] == value, packed, zero) for value in group_ids],
            axis=0,
        )
        spots = lax.dot_general(
            masked, onehot, (((1,), (1,)), ((), ())), preferred_element_type=F32
        ).astype(jnp.int32)
        for group in range(2 * groups):
            piece = spots[group * rows : (group + 1) * rows]
            for part in range(PACK):
                at = (copy + 1) * snp_rows + part * rows
                picked[at : at + rows, group * LANES : (group + 1) * LANES] = (
                    lax.shift_right_logical(piece, 2 * part) & 3
                ).astype(F32).astype(BF16)
    picked[:snp_rows, :block] = dose[0].astype(F32).astype(BF16)
    picked[:snp_rows, block:] = dose[1].astype(F32).astype(BF16)
    all_rows = copies * snp_rows
    picked[all_rows:, :] = jnp.ones((picked.shape[0] - all_rows, 2 * block), BF16)
    row_sum = jnp.sum(picked[:all_rows].astype(F32), axis=1, keepdims=True)
    mean_rows = jnp.concatenate([dose_mean] * copies, axis=0)
    inv_rows = jnp.concatenate([inv_spread] * copies, axis=0)
    excess = row_sum - mean_rows * (2.0 * block)
    scaled_excess = excess * inv_rows
    excess_ref[...] = scaled_excess[snp_rows:]
    first_excess_ref[...] = scaled_excess[:snp_rows]
    spot = lax.broadcasted_iota(jnp.int32, (snp_rows, snp_rows), 0)
    diagonal = spot == lax.broadcasted_iota(jnp.int32, (snp_rows, snp_rows), 1)
    weight = jnp.sum(jnp.where(diagonal, weight_ref[...], 0.0), axis=1, keepdims=True)
    spread_weight_ref[...] = jnp.broadcast_to(weight, spread_weight_ref.shape)
    for fetch in fetches:
        fetch.wait()
    start = 0
    for chunk_ref in chunk_refs:
        cols = slice(start, start + chunk_ref.shape[1])
        raw = jnp.dot(picked[...], genes[:, cols], preferred_element_type=F32)
        total = raw[all_rows : all_rows + 1]
        mean = total / (2.0 * block)
        part = (raw[:all_rows] - mean_rows * total - mean * excess) * inv_rows
        part = part.astype(BF16)
        chunk_ref[...] = part[snp_rows:]
        first_ref[:, cols] = part[:snp_rows]
        mean_ref[:, cols] = mean
        start = cols.stop


def gram_kernel(pieces, *refs):
    chunks = len(CHUNK_LANES)
    inputs = refs[: 2 * chunks]
    weight_ref = refs[2 * chunks]
    rest = refs[2 * chunks + 1 :]
    held, sems = rest[-2:]
    rows = inputs[0].shape[0]
    copies = []
    start = 0
    for place, source in enumerate(inputs):
        copies.append(
            pltpu.make_async_copy(
                source, held.at[:, pl.ds(start, source.shape[1])], sems.at[place]
            )
        )
        copies[-1].start()
        start += source.shape[1]
    weight = jnp.concatenate([weight_ref[:, :1]] * (rows // weight_ref.shape[0]), axis=0)
    for copy in copies:
        copy.wait()
    samp = lax.axis_index("samp")
    snp = lax.axis_index("snp")
    width = held.shape[1] // BLOCKS
    first = ((samp // 2) * 2 + lax.rem(snp, 2)) * 2
    depth = snp // 2
    own = held[:, pl.ds(pl.multiple_of(first * width, width), 2 * width)].astype(F32)
    turned = (own * weight).T.astype(BF16)
    images = []
    for line in range(2):
        at = pl.ds(pl.multiple_of((first + line) * width, width), REACH * width)
        images.append(
            jnp.dot(
                turned[line * width : (line + 1) * width],
                held[:, at],
                preferred_element_type=F32,
            )
        )
    if pieces is None:
        strip_ref = rest[0]
        for line in range(2):
            strip_ref[line * width : (line + 1) * width, :] = images[line]
        return
    strip_ref, strip = rest[0], rest[-3]
    outs = rest[1:-3]
    for line in range(2):
        at = slice(line * width, (line + 1) * width)
        strip[at, :] = strip_ref[at, :] + images[line]
    size = 2 * width // pieces
    for step in range(pieces):
        at = lax.bitwise_xor(depth, step) * size
        outs[step][...] = strip[pl.ds(pl.multiple_of(at, size), size), :].astype(BF16)


def chain_kernel(pieces, total_rows, *refs):
    chunks = len(CHUNK_LANES)
    groups = min(GROUPS, pieces)
    strips = refs[: 8 * groups]
    nulls = refs[8 * groups : 8 * groups + 2 * chunks]
    firsts = refs[8 * groups + 2 * chunks : 8 * groups + 2 * chunks + 2]
    out_ref, matrix, kept, current, sems = refs[8 * groups + 2 * chunks + 2 :]
    samp = lax.axis_index("samp")
    snp = lax.axis_index("snp")
    core = lax.rem(samp, 2)
    side = samp // 2
    minor = lax.rem(snp, 2)
    depth = snp // 2
    genes = matrix.shape[0]
    width = genes // BLOCKS
    size = 2 * width // pieces
    reach = REACH * width
    null_rows = nulls[0].shape[0] // 2
    first_rows = kept.shape[0] - null_rows
    for place, source in enumerate(strips):
        flips, group = divmod(place, groups)
        block = (
            flip_bit(core, flips // 4) * 8
            + flip_bit(side, flips // 2 % 2) * 4
            + flip_bit(minor, flips % 2) * 2
        )
        for inner in range(pieces // groups):
            piece = lax.bitwise_xor(depth, group * (pieces // groups) + inner)
            row = pl.multiple_of(block * width + piece * size, size)
            column = pl.multiple_of((row // width) * width, width)
            pltpu.make_async_copy(
                source.at[pl.ds(inner * size, size), :],
                matrix.at[pl.ds(row, size), pl.ds(column, reach)],
                sems.at[0],
            ).start()
    half = genes // 2
    for flip in range(2):
        holder = flip_bit(core, flip)
        start = 0
        for chunk in range(chunks):
            source = nulls[flip * chunks + chunk]
            column = pl.multiple_of(holder * half + start, LANES)
            pltpu.make_async_copy(
                source.at[pl.ds(pl.multiple_of(core * null_rows, null_rows), null_rows), :],
                kept.at[pl.ds(0, null_rows), pl.ds(column, source.shape[1])],
                sems.at[1],
            ).start()
            start += source.shape[1]
        skip = firsts[0].shape[0] - first_rows
        pltpu.make_async_copy(
            firsts[flip].at[pl.ds(pl.multiple_of(core * skip, 16), first_rows), :],
            kept.at[
                pl.ds(null_rows, first_rows), pl.ds(pl.multiple_of(holder * half, half), half)
            ],
            sems.at[1],
        ).start()
    filled = matrix.at[:, pl.ds(0, reach)]
    pltpu.make_async_copy(filled, filled, sems.at[0]).wait()
    pltpu.make_async_copy(kept, kept, sems.at[1]).wait()

    trace = jnp.zeros((1, 1), F32)
    eye = lax.broadcasted_iota(jnp.int32, (width, width), 0) == lax.broadcasted_iota(
        jnp.int32, (width, width), 1
    )
    diagonal = jnp.zeros((width, width), F32)
    for block in range(BLOCKS):
        at = slice(block * width, (block + 1) * width)
        diagonal = diagonal + jnp.where(eye, matrix[at, at].astype(F32), 0.0)
    trace = jnp.sum(jnp.sum(diagonal, axis=1, keepdims=True), axis=0, keepdims=True)
    scale = trace / total_rows / genes + 1e-06
    factor = 0.5 / (total_rows * scale)

    for block in range(BLOCKS):
        over = block + REACH - BLOCKS
        if over > 0:
            at = slice(block * width, (block + 1) * width)
            matrix[at, : over * width] = matrix[at, genes : genes + over * width]

    def mirror(block, carry):
        home = pl.ds(pl.multiple_of(block * width, width), width)
        for step in range(1, REACH - 1):
            at = pl.ds(pl.multiple_of((block + step) * width, width), width)
            target = pl.multiple_of(lax.rem(block + step, BLOCKS) * width, width)
            matrix[pl.ds(target, width), home] = matrix[home, at].T
        return carry

    lax.fori_loop(0, BLOCKS, mirror, 0)
    wide = 2 * width

    def apply(source, target):
        def one(block, carry):
            at = pl.ds(pl.multiple_of(block * wide, wide), wide)
            image = jnp.dot(source[...], matrix[:, at], preferred_element_type=F32)
            target[:, at] = (1.5 * source[:, at].astype(F32) - factor * image).astype(BF16)
            return carry

        lax.fori_loop(0, genes // wide, one, 0)

    first_image, second_image = current.at[0], current.at[1]
    apply(kept, first_image)
    apply(first_image, second_image)
    apply(second_image, kept)
    inverse = lax.rsqrt(scale)
    quarter = genes // 4
    for flip in range(2):
        base = side * half + flip_bit(core, flip) * quarter
        for inner in range(quarter // wide):
            at = pl.ds(pl.multiple_of(base + inner * wide, wide), wide)
            image = jnp.dot(kept[...], matrix[:, at], preferred_element_type=F32)
            value = (1.5 * first_image[:, at].astype(F32) - factor * image) * inverse
            out_ref[flip, :, inner * wide : (inner + 1) * wide] = value.astype(BF16)


def shards(samp_count, snp_count, dosage, pheno, perm, snp_weight):
    snp_rows, block = dosage.shape
    genes = pheno.shape[1]
    total_samples = block * samp_count
    total_snps = snp_rows * snp_count
    null_count = perm.shape[0]
    copies = null_count + 1
    half = genes // 2
    width = genes // BLOCKS
    chunk_cols = [half * lanes // sum(CHUNK_LANES) for lanes in CHUNK_LANES]
    chunks = len(chunk_cols)
    null_rows = null_count * snp_rows
    pieces = snp_count // 2
    size = 2 * width // pieces
    groups = min(GROUPS, pieces)
    move = functools.partial(permute, samp_count=samp_count, snp_count=snp_count)
    over_core = functools.partial(move, move=lambda a, b: (a ^ 1, b))
    over_side = functools.partial(move, move=lambda a, b: (a ^ 2, b))
    over_both = functools.partial(move, move=lambda a, b: (a ^ 3, b))
    over_minor = functools.partial(move, move=lambda a, b: (a, b ^ 1))

    def over_depth(value, step):
        return move(value, move=lambda a, b: (a, b ^ (2 * step)))

    core = lax.axis_index("samp") % 2
    small = jnp.concatenate([dosage, perm], axis=0).astype(jnp.int16)
    smalls = [small, over_core(small), over_side(small), over_both(small)]
    mate_pheno = over_core(pheno)

    all_rows = copies * snp_rows
    shape = jax.ShapeDtypeStruct
    parts = pl.pallas_call(
        functools.partial(score_kernel, copies, snp_rows, block, half, float(total_samples)),
        out_shape=[shape((null_rows, cols), BF16) for cols in chunk_cols]
        + [
            shape((snp_rows, half), BF16),
            shape((1, half), F32),
            shape((null_rows, 1), F32),
            shape((snp_rows, 1), F32),
            shape((snp_rows, LANES), F32),
        ],
        in_specs=[VMEM] * 4 + [ANY, ANY, VMEM],
        out_specs=[VMEM] * (chunks + 5),
        scratch_shapes=[
            pltpu.VMEM((all_rows + 16, 2 * block), BF16),
            pltpu.VMEM((2 * block, half), BF16),
            pltpu.SemaphoreType.DMA((2,)),
        ],
        name="score",
    )(*smalls, pheno, mate_pheno, snp_weight.reshape(1, snp_rows))
    partial_first, mean, excess, first_excess, weight = parts[chunks:]
    shift = mean - over_side(mean)
    mate_weight = over_minor(weight)

    def finish(value, offset, rows):
        both = value.astype(F32) + over_side(value).astype(F32)
        return (both + offset * rows).astype(BF16)

    own = []
    start = 0
    for value in parts[:chunks]:
        stop = start + value.shape[1]
        own.append(finish(value, shift[:, start:stop], excess))
        start = stop
    own_first = finish(partial_first, shift, first_excess)
    mate = [over_core(value) for value in own]
    minor = [over_minor(value) for value in own]
    minor_mate = [over_core(value) for value in minor]
    mate_first = over_core(own_first)

    strip = pl.pallas_call(
        functools.partial(gram_kernel, None),
        out_shape=shape((2 * width, REACH * width), F32),
        in_specs=[ANY] * (2 * chunks) + [VMEM],
        out_specs=VMEM,
        scratch_shapes=[
            pltpu.VMEM((null_rows, genes), BF16),
            pltpu.SemaphoreType.DMA((2 * chunks,)),
        ],
        name="gram_own",
    )(*own, *mate, weight)
    strips = pl.pallas_call(
        functools.partial(gram_kernel, pieces),
        out_shape=[shape((size, REACH * width), BF16)] * pieces,
        in_specs=[ANY] * (2 * chunks) + [VMEM] * 2,
        out_specs=[VMEM] * pieces,
        scratch_shapes=[
            pltpu.VMEM((2 * width, REACH * width), F32),
            pltpu.VMEM((null_rows, genes), BF16),
            pltpu.SemaphoreType.DMA((2 * chunks,)),
        ],
        name="gram_minor",
    )(*minor, *minor_mate, mate_weight, strip)

    piece = strips[0].astype(F32)
    for step in range(1, pieces):
        piece = piece + over_depth(strips[step], step).astype(F32)
    piece = piece.astype(BF16)
    line = [piece] + [over_depth(piece, step) for step in range(1, pieces)]
    inner = pieces // groups
    if inner > 1:
        line = [
            jnp.concatenate(line[group * inner : (group + 1) * inner], axis=0)
            for group in range(groups)
        ]
    side = [over_side(value) for value in line]
    across = [over_minor(value) for value in line]
    far = [
        over_side(across[group]) if group % 2 else over_minor(side[group])
        for group in range(groups)
    ]
    plane = [*line, *across, *side, *far]
    plane_mate = [over_core(value) for value in plane]

    first_rows = 32
    work_rows = null_rows // 2 + first_rows
    result = pl.pallas_call(
        functools.partial(chain_kernel, pieces, float(null_count * total_snps)),
        out_shape=shape((2, work_rows, genes // samp_count), BF16),
        in_specs=[ANY] * (8 * groups + 2 * chunks + 2),
        out_specs=VMEM,
        scratch_shapes=[
            pltpu.VMEM((genes, (BLOCKS + REACH - 1) * width), BF16),
            pltpu.VMEM((work_rows, genes), BF16),
            pltpu.VMEM((2, work_rows, genes), BF16),
            pltpu.SemaphoreType.DMA((2,)),
        ],
        name="chain",
    )(*plane, *plane_mate, *own, *mate, own_first, mate_first)

    mine = result[0]
    theirs = over_core(result[1])
    low = jnp.where(core == 0, mine, theirs)
    high = jnp.where(core == 0, theirs, mine)
    half_null = null_rows // 2
    spare = 2 * first_rows - snp_rows
    white = jnp.concatenate(
        [
            low[half_null:],
            high[half_null + spare :],
            low[:half_null],
            high[:half_null],
        ],
        axis=0,
    )
    return white.reshape(copies, snp_rows, genes // samp_count)


def solution(mesh):
    return jax.shard_map(
        functools.partial(shards, mesh.shape["samp"], mesh.shape["snp"]),
        mesh=mesh,
        in_specs=(P("snp", "samp"), P("samp", None), P(None, "samp"), P("snp")),
        out_specs=P(None, "snp", "samp"),
        check_vma=False,
    )
```

```python
import functools

import jax
import jax.numpy as jnp
from jax import lax
from jax.experimental import pallas as pl
from jax.experimental.pallas import tpu as pltpu
from jax.sharding import PartitionSpec as P


LANES = 128
PACK = 3
BLOCKS = 16
REACH = 9
CHUNK_LANES = (1, 2, 2, 2, 1)
GROUPS = 4
TOTAL_STEPS = 64.0
CENTER_SHARE = 8
AXES = ("samp", "snp")


def limit(mebibytes):
    return pltpu.CompilerParams(vmem_limit_bytes=mebibytes * 2**20)


ANY = pl.BlockSpec(memory_space=pl.ANY)
HBM = pl.BlockSpec(memory_space=pltpu.HBM)
VMEM = pl.BlockSpec(memory_space=pltpu.VMEM)
BF16 = jnp.bfloat16
F32 = jnp.float32


def permute(value, samp_count, snp_count, move):
    pairs = []
    for samp in range(samp_count):
        for snp in range(snp_count):
            samp_to, snp_to = move(samp, snp)
            pairs.append((samp * snp_count + snp, samp_to * snp_count + snp_to))
    return lax.ppermute(value, AXES, pairs)


def flip_bit(value, flip):
    return value + flip - 2 * value * flip


def pack_kernel(dosage_ref, perm_ref, pheno_ref, out_ref, sample, dosage, perm, sems):
    block = dosage_ref.shape[1]
    fetches = [
        pltpu.make_async_copy(dosage_ref, dosage, sems.at[0]),
        pltpu.make_async_copy(perm_ref, perm, sems.at[1]),
        pltpu.make_async_copy(pheno_ref.at[pl.ds(0, sample.shape[0]), :], sample, sems.at[2]),
    ]
    for fetch in fetches:
        fetch.start()
    for fetch in fetches:
        fetch.wait()
    ones = jnp.ones((16, sample.shape[0]), BF16)
    total = jnp.dot(ones, sample[...], preferred_element_type=F32)[:1]
    steps = jnp.round(total * TOTAL_STEPS).astype(jnp.int32)
    lines = [steps[:, at : at + block] for at in range(0, steps.shape[1], block)]
    fill = -(len(lines) + dosage.shape[0] + perm.shape[0]) % 16
    lines += [jnp.zeros((fill, block), jnp.int32)] if fill else []
    out_ref[...] = jnp.concatenate([dosage[...], perm[...], *lines], axis=0).astype(
        jnp.int16
    )


def join_kernel(first_rows, spare, mine_ref, theirs_ref, out_ref, held, sems):
    core = lax.rem(lax.axis_index("samp"), 2)
    fetches = [
        pltpu.make_async_copy(source, held.at[place], sems.at[place])
        for place, source in enumerate((mine_ref, theirs_ref))
    ]
    for fetch in fetches:
        fetch.start()
    for fetch in fetches:
        fetch.wait()
    mine, theirs = held[0], held[1]
    low = jnp.where(core == 0, mine, theirs)
    high = jnp.where(core == 0, theirs, mine)
    nulls = mine.shape[0] - first_rows
    at = first_rows
    out_ref[:at] = low[nulls:]
    out_ref[at : at + first_rows - spare] = high[nulls + spare :]
    at += first_rows - spare
    out_ref[at : at + nulls] = low[:nulls]
    out_ref[at + nulls :] = high[:nulls]


def score_kernel(copies, snp_rows, block, half, total_samples, *refs):
    smalls = refs[0:4]
    pheno_ref, mate_ref, weight_ref = refs[4:7]
    chunks = len(CHUNK_LANES)
    chunk_refs = refs[7 : 7 + chunks]
    first_ref, spread_weight_ref = refs[7 + chunks : -4]
    picked, genes, held, sems = refs[-4:]
    samp = lax.axis_index("samp")
    core = lax.rem(samp, 2)
    mate = flip_bit(core, 1) - core + samp
    own_cols = pl.ds(pl.multiple_of(core * half, half), half)
    fetches = [
        pltpu.make_async_copy(
            source.at[:, own_cols], genes.at[pl.ds(place * block, block), :], sems.at[place]
        )
        for place, source in enumerate((pheno_ref, mate_ref))
    ]
    fetches += [
        pltpu.make_async_copy(small, held.at[place], sems.at[2 + place])
        for place, small in enumerate(smalls)
    ]
    for fetch in fetches:
        fetch.start()
    for fetch in fetches[2:]:
        fetch.wait()
    nulls = copies - 1
    loaded = [held[place].astype(jnp.int32) for place in range(4)]
    dose = [value[:snp_rows] for value in loaded]
    perm = jnp.concatenate([value[snp_rows : snp_rows + nulls] for value in loaded], axis=1)
    steps = loaded[0] + loaded[1] + loaded[2] + loaded[3]
    at = snp_rows + nulls
    lines = half // block
    center = jnp.concatenate(
        [
            jnp.where(core == 0, steps[at + line], steps[at + lines + line]).reshape(1, block)
            for line in range(lines)
        ],
        axis=1,
    ).astype(F32) * (CENTER_SHARE / (TOTAL_STEPS * total_samples))
    dose_all = jnp.concatenate(dose, axis=1)
    rows = snp_rows // PACK
    packed = dose_all[:rows]
    for part in range(1, PACK):
        packed = packed + dose_all[part * rows : (part + 1) * rows] * (4**part)
    packed = packed.astype(F32).astype(BF16)
    dose_float = dose_all.astype(F32)
    dose_mean = jnp.sum(dose_float, axis=1, keepdims=True) / total_samples
    dose_square = jnp.sum(dose_float * dose_float, axis=1, keepdims=True) / total_samples
    inv_spread = lax.rsqrt(total_samples * (dose_square + 1e-05))
    groups = block // LANES
    high = (perm // LANES).astype(F32).astype(BF16)
    low = (perm % LANES).astype(F32).astype(BF16)
    lane_ids = lax.broadcasted_iota(jnp.int32, (LANES, dose_all.shape[1]), 0)
    lane_ids = lane_ids.astype(F32).astype(BF16)
    one = jnp.ones((), BF16)
    zero = jnp.zeros((), BF16)
    group_ids = [samp * groups + group for group in range(groups)]
    group_ids += [mate * groups + group for group in range(groups)]
    group_ids = [value.astype(F32).astype(BF16) for value in group_ids]
    for copy in range(nulls):
        onehot = jnp.where(lane_ids == low[copy : copy + 1], one, zero)
        masked = jnp.concatenate(
            [jnp.where(high[copy : copy + 1] == value, packed, zero) for value in group_ids],
            axis=0,
        )
        spots = lax.dot_general(
            masked, onehot, (((1,), (1,)), ((), ())), preferred_element_type=F32
        ).astype(jnp.int32)
        for group in range(2 * groups):
            piece = spots[group * rows : (group + 1) * rows]
            for part in range(PACK):
                at = (copy + 1) * snp_rows + part * rows
                picked[at : at + rows, group * LANES : (group + 1) * LANES] = (
                    lax.shift_right_logical(piece, 2 * part) & 3
                ).astype(F32).astype(BF16)
    picked[:snp_rows, :block] = dose[0].astype(F32).astype(BF16)
    picked[:snp_rows, block:] = dose[1].astype(F32).astype(BF16)
    all_rows = copies * snp_rows
    picked[all_rows:, :] = jnp.ones((picked.shape[0] - all_rows, 2 * block), BF16)
    row_sum = jnp.sum(picked[:all_rows].astype(F32), axis=1, keepdims=True)
    mean_rows = jnp.concatenate([dose_mean] * copies, axis=0)
    inv_rows = jnp.concatenate([inv_spread] * copies, axis=0)
    excess = row_sum - mean_rows * (2.0 * block)
    spot = lax.broadcasted_iota(jnp.int32, (snp_rows, snp_rows), 0)
    diagonal = spot == lax.broadcasted_iota(jnp.int32, (snp_rows, snp_rows), 1)
    weight = jnp.sum(jnp.where(diagonal, weight_ref[...], 0.0), axis=1, keepdims=True)
    spread_weight_ref[...] = jnp.broadcast_to(weight, spread_weight_ref.shape)
    for fetch in fetches[:2]:
        fetch.wait()
    raw = jnp.dot(picked[...], genes[...], preferred_element_type=F32)
    total = raw[all_rows : all_rows + 1]
    part = ((raw[:all_rows] - mean_rows * total - center * excess) * inv_rows).astype(BF16)
    first_ref[...] = part[:snp_rows]
    start = 0
    for chunk_ref in chunk_refs:
        stop = start + chunk_ref.shape[1]
        chunk_ref[...] = part[snp_rows:, start:stop]
        start = stop


def gram_kernel(pieces, *refs):
    chunks = len(CHUNK_LANES)
    inputs = refs[: 4 * chunks]
    weight_refs = refs[4 * chunks : 4 * chunks + 2]
    outs = refs[4 * chunks + 2 : -3]
    strip, held, sems = refs[-3:]
    rows = inputs[0].shape[0]
    copies = []
    for slab in range(2):
        start = 0
        for place in range(slab * 2 * chunks, (slab + 1) * 2 * chunks):
            source = inputs[place]
            copies.append(
                pltpu.make_async_copy(
                    source,
                    held.at[pl.ds(slab * rows, rows), pl.ds(start, source.shape[1])],
                    sems.at[place],
                )
            )
            copies[-1].start()
            start += source.shape[1]
    weight = jnp.concatenate(
        [
            weight_ref[:, :1]
            for weight_ref in weight_refs
            for _ in range(rows // weight_ref.shape[0])
        ],
        axis=0,
    )
    for copy in copies:
        copy.wait()
    samp = lax.axis_index("samp")
    snp = lax.axis_index("snp")
    width = held.shape[1] // BLOCKS
    first = ((samp // 2) * 2 + lax.rem(snp, 2)) * 2
    depth = snp // 2
    own = held[:, pl.ds(pl.multiple_of(first * width, width), 2 * width)].astype(F32)
    turned = (own * weight).T.astype(BF16)
    span = (REACH + 1) * width
    cover = held[:, pl.ds(pl.multiple_of(first * width, 2 * width), span)]
    image = jnp.dot(turned, cover, preferred_element_type=F32)
    for line in range(2):
        strip[line * width : (line + 1) * width, :] = image[
            line * width : (line + 1) * width, line * width : (line + REACH) * width
        ]
    size = 2 * width // pieces
    for step in range(pieces):
        at = lax.bitwise_xor(depth, step) * size
        outs[step][...] = strip[pl.ds(pl.multiple_of(at, size), size), :].astype(BF16)


def chain_kernel(pieces, total_rows, *refs):
    chunks = len(CHUNK_LANES)
    groups = GROUPS
    strips = refs[: 8 * groups]
    nulls = refs[8 * groups : 8 * groups + 2 * chunks]
    firsts = refs[8 * groups + 2 * chunks : 8 * groups + 2 * chunks + 2]
    own_ref, mate_ref, matrix, kept, current, sems = refs[8 * groups + 2 * chunks + 2 :]
    samp = lax.axis_index("samp")
    snp = lax.axis_index("snp")
    core = lax.rem(samp, 2)
    side = samp // 2
    minor = lax.rem(snp, 2)
    depth = snp // 2
    genes = matrix.shape[0]
    width = genes // BLOCKS
    size = 2 * width // pieces
    reach = REACH * width
    null_rows = nulls[0].shape[0] // 2
    first_rows = kept.shape[0] - null_rows
    for place, source in enumerate(strips):
        flips, group = divmod(place, groups)
        block = (
            flip_bit(core, flips // 4) * 8
            + flip_bit(side, flips // 2 % 2) * 4
            + flip_bit(minor, flips % 2) * 2
        )
        for inner in range(pieces // groups):
            piece = lax.bitwise_xor(depth, group * (pieces // groups) + inner)
            row = pl.multiple_of(block * width + piece * size, size)
            column = pl.multiple_of((row // width) * width, width)
            pltpu.make_async_copy(
                source.at[pl.ds(inner * size, size), :],
                matrix.at[pl.ds(row, size), pl.ds(column, reach)],
                sems.at[0],
            ).start()
    half = genes // 2
    for flip in range(2):
        holder = flip_bit(core, flip)
        start = 0
        for chunk in range(chunks):
            source = nulls[flip * chunks + chunk]
            column = pl.multiple_of(holder * half + start, LANES)
            pltpu.make_async_copy(
                source.at[pl.ds(pl.multiple_of(core * null_rows, null_rows), null_rows), :],
                kept.at[pl.ds(0, null_rows), pl.ds(column, source.shape[1])],
                sems.at[1],
            ).start()
            start += source.shape[1]
        skip = firsts[0].shape[0] - first_rows
        pltpu.make_async_copy(
            firsts[flip].at[pl.ds(pl.multiple_of(core * skip, 16), first_rows), :],
            kept.at[
                pl.ds(null_rows, first_rows), pl.ds(pl.multiple_of(holder * half, half), half)
            ],
            sems.at[1],
        ).start()
    filled = matrix.at[:, pl.ds(0, reach)]
    pltpu.make_async_copy(filled, filled, sems.at[0]).wait()
    pltpu.make_async_copy(kept, kept, sems.at[1]).wait()

    trace = jnp.zeros((1, 1), F32)
    eye = lax.broadcasted_iota(jnp.int32, (width, width), 0) == lax.broadcasted_iota(
        jnp.int32, (width, width), 1
    )
    diagonal = jnp.zeros((width, width), F32)
    for block in range(BLOCKS):
        at = slice(block * width, (block + 1) * width)
        diagonal = diagonal + jnp.where(eye, matrix[at, at].astype(F32), 0.0)
    trace = jnp.sum(jnp.sum(diagonal, axis=1, keepdims=True), axis=0, keepdims=True)
    scale = trace / total_rows / genes + 1e-06
    factor = 0.5 / (total_rows * scale)

    for block in range(BLOCKS):
        over = block + REACH - BLOCKS
        if over > 0:
            at = slice(block * width, (block + 1) * width)
            matrix[at, : over * width] = matrix[at, genes : genes + over * width]

    for block in range(BLOCKS):
        home = slice(block * width, (block + 1) * width)
        turned = matrix[home, (block + 1) * width : (block + REACH - 1) * width].T
        for step in range(1, REACH - 1):
            target = (block + step) % BLOCKS * width
            matrix[target : target + width, home] = turned[(step - 1) * width : step * width]

    def apply(source, target):
        image = jnp.dot(source[...], matrix[:, :genes], preferred_element_type=F32)
        target[...] = (1.5 * source[...].astype(F32) - factor * image).astype(BF16)

    first_image, second_image = current.at[0], current.at[1]
    apply(kept, first_image)
    apply(first_image, second_image)
    apply(second_image, kept)
    inverse = lax.rsqrt(scale)
    at = pl.ds(pl.multiple_of(side * half, half), half)
    image = jnp.dot(kept[...], matrix[:, at], preferred_element_type=F32)
    value = (1.5 * first_image[:, at].astype(F32) - factor * image) * inverse
    second_image[:, :half] = value.astype(BF16)
    quarter = half // 2
    for flip, out_ref in enumerate((own_ref, mate_ref)):
        base = pl.multiple_of(flip_bit(core, flip) * quarter, quarter)
        out_ref[...] = second_image[:, pl.ds(base, quarter)]


def shards(samp_count, snp_count, dosage, pheno, perm, snp_weight):
    snp_rows, block = dosage.shape
    genes = pheno.shape[1]
    total_samples = block * samp_count
    total_snps = snp_rows * snp_count
    null_count = perm.shape[0]
    copies = null_count + 1
    half = genes // 2
    width = genes // BLOCKS
    chunk_cols = [half * lanes // sum(CHUNK_LANES) for lanes in CHUNK_LANES]
    chunks = len(chunk_cols)
    null_rows = null_count * snp_rows
    pieces = snp_count // 2
    size = 2 * width // pieces
    groups = GROUPS

    def move(value, step):
        return permute(value, samp_count, snp_count, step)

    def over_core(value):
        return move(value, lambda a, b: (a ^ 1, b))

    def over_side(value):
        return move(value, lambda a, b: (a ^ 2, b))

    def over_both(value):
        return move(value, lambda a, b: (a ^ 3, b))

    def over_minor(value):
        return move(value, lambda a, b: (a, b ^ 1))

    def over_plane(value):
        return move(value, lambda a, b: (a ^ 2, b ^ 1))

    def over_depth(value, step):
        return move(value, lambda a, b: (a, b ^ (2 * step)))

    small_rows = snp_rows + null_count + genes // block
    small_rows += -small_rows % 16
    small = pl.pallas_call(
        pack_kernel,
        out_shape=jax.ShapeDtypeStruct((small_rows, block), jnp.int16),
        in_specs=[HBM] * 3,
        out_specs=VMEM,
        scratch_shapes=[
            pltpu.VMEM((block // CENTER_SHARE, genes), BF16),
            pltpu.VMEM(dosage.shape, jnp.int32),
            pltpu.VMEM(perm.shape, jnp.int32),
            pltpu.SemaphoreType.DMA((3,)),
        ],
        compiler_params=limit(60),
        name="pack",
    )(dosage, perm, pheno)
    smalls = [small, over_core(small), over_side(small), over_both(small)]
    mate_pheno = over_core(pheno)

    all_rows = copies * snp_rows
    shape = jax.ShapeDtypeStruct
    parts = pl.pallas_call(
        functools.partial(score_kernel, copies, snp_rows, block, half, float(total_samples)),
        out_shape=[shape((null_rows, cols), BF16) for cols in chunk_cols]
        + [
            shape((snp_rows, half), BF16),
            shape((snp_rows, LANES), F32),
        ],
        in_specs=[HBM] + [ANY] * 5 + [VMEM],
        out_specs=[VMEM] * (chunks + 2),
        scratch_shapes=[
            pltpu.VMEM((all_rows + 16, 2 * block), BF16),
            pltpu.VMEM((2 * block, half), BF16),
            pltpu.VMEM((4, *small.shape), jnp.int16),
            pltpu.SemaphoreType.DMA((6,)),
        ],
        compiler_params=limit(20),
        name="score",
    )(*smalls, pheno, mate_pheno, snp_weight.reshape(1, snp_rows))
    partial_first, weight = parts[chunks:]
    mate_weight = over_minor(weight)

    def finish(value):
        return (value.astype(F32) + over_side(value).astype(F32)).astype(BF16)

    own = [finish(value) for value in parts[:chunks]]
    own_first = finish(partial_first)
    mate = [over_core(value) for value in own]
    minor = [over_minor(value) for value in own]
    minor_mate = [over_core(value) for value in minor]
    mate_first = over_core(own_first)

    strips = pl.pallas_call(
        functools.partial(gram_kernel, pieces),
        out_shape=[shape((size, REACH * width), BF16)] * pieces,
        in_specs=[ANY] * (4 * chunks) + [VMEM] * 2,
        out_specs=[VMEM] * pieces,
        scratch_shapes=[
            pltpu.VMEM((2 * width, REACH * width), F32),
            pltpu.VMEM((2 * null_rows, genes), BF16),
            pltpu.SemaphoreType.DMA((4 * chunks,)),
        ],
        compiler_params=limit(20),
        name="gram",
    )(*own, *mate, *minor, *minor_mate, weight, mate_weight)

    piece = strips[0].astype(F32)
    for step in range(1, pieces):
        piece = piece + over_depth(strips[step], step).astype(F32)
    held = {0: piece.astype(BF16)}
    inner = pieces // groups
    bit = inner // 2
    while bit:
        for step in sorted(held):
            held[step + bit] = over_depth(held[step], bit)
        bit //= 2
    base = jnp.concatenate([held[step] for step in range(inner)], axis=0)
    plane = {}
    for far in (0, 2):
        near = far + 1
        at = over_depth(base, 2 * inner) if far else base
        plane[0, 0, far] = at
        plane[0, 0, near] = over_depth(at, inner)
        plane[1, 0, far] = over_side(at)
        plane[0, 1, far] = over_minor(at)
        plane[0, 1, near] = over_minor(plane[0, 0, near])
        plane[1, 0, near] = over_depth(plane[1, 0, far], inner)
        plane[1, 1, far] = over_side(plane[0, 1, far])
        plane[1, 1, near] = (
            over_plane(plane[0, 0, near])
            if far
            else over_minor(plane[1, 0, near])
        )
    places = [
        (side, minor, group) for side in range(2) for minor in range(2) for group in range(groups)
    ]
    plane_mate = [over_core(plane[place]) for place in places]
    plane = [plane[place] for place in places]

    first_rows = 32
    work_rows = null_rows // 2 + first_rows
    mine, other = pl.pallas_call(
        functools.partial(chain_kernel, pieces, float(null_count * total_snps)),
        out_shape=[shape((work_rows, genes // samp_count), BF16)] * 2,
        in_specs=[ANY] * (8 * groups + 2 * chunks + 2),
        out_specs=[VMEM] * 2,
        scratch_shapes=[
            pltpu.VMEM((genes, (BLOCKS + REACH - 1) * width), BF16),
            pltpu.VMEM((work_rows, genes), BF16),
            pltpu.VMEM((2, work_rows, genes), BF16),
            pltpu.SemaphoreType.DMA((2,)),
        ],
        compiler_params=limit(28),
        name="chain",
    )(*plane, *plane_mate, *own, *mate, own_first, mate_first)
    theirs = over_core(other)
    white = pl.pallas_call(
        functools.partial(join_kernel, first_rows, 2 * first_rows - snp_rows),
        out_shape=shape((all_rows, genes // samp_count), BF16),
        in_specs=[ANY] * 2,
        out_specs=VMEM,
        scratch_shapes=[
            pltpu.VMEM((2, *mine.shape), BF16),
            pltpu.SemaphoreType.DMA((2,)),
        ],
        compiler_params=limit(8),
        name="join",
    )(mine, theirs)
    return white.reshape(copies, snp_rows, genes // samp_count)


def layer(samp_count, snp_count, *args):
    return shards(samp_count, snp_count, *args)


def solution(mesh):
    samp_count, snp_count = mesh.shape["samp"], mesh.shape["snp"]
    return jax.shard_map(
        functools.partial(layer, samp_count, snp_count),
        mesh=mesh,
        in_specs=(P("snp", "samp"), P("samp", None), P(None, "samp"), P("snp")),
        out_specs=P(None, "snp", "samp"),
        check_vma=False,
    )
```

```python
import functools

import jax
import jax.numpy as jnp
from jax import lax
from jax.experimental import pallas as pl
from jax.experimental.pallas import tpu as pltpu
from jax.sharding import PartitionSpec as P


LANES = 128
PACK = 3
BLOCKS = 16
REACH = 9
CHUNK_LANES = (1, 2, 2, 2, 1)
GROUPS = 4
TOTAL_STEPS = 64.0
CENTER_SHARE = 8
AXES = ("samp", "snp")


def limit(mebibytes):
    return pltpu.CompilerParams(vmem_limit_bytes=mebibytes * 2**20)


ANY = pl.BlockSpec(memory_space=pl.ANY)
HBM = pl.BlockSpec(memory_space=pltpu.HBM)
VMEM = pl.BlockSpec(memory_space=pltpu.VMEM)
BF16 = jnp.bfloat16
F32 = jnp.float32


def permute(value, samp_count, snp_count, move):
    pairs = []
    for samp in range(samp_count):
        for snp in range(snp_count):
            samp_to, snp_to = move(samp, snp)
            pairs.append((samp * snp_count + snp, samp_to * snp_count + snp_to))
    return lax.ppermute(value, AXES, pairs)


def flip_bit(value, flip):
    return value + flip - 2 * value * flip


def pack_kernel(dosage_ref, perm_ref, pheno_ref, out_ref, sample, dosage, perm, sems):
    block = dosage_ref.shape[1]
    fetches = [
        pltpu.make_async_copy(dosage_ref, dosage, sems.at[0]),
        pltpu.make_async_copy(perm_ref, perm, sems.at[1]),
        pltpu.make_async_copy(pheno_ref.at[pl.ds(0, sample.shape[0]), :], sample, sems.at[2]),
    ]
    for fetch in fetches:
        fetch.start()
    for fetch in fetches:
        fetch.wait()
    ones = jnp.ones((16, sample.shape[0]), BF16)
    total = jnp.dot(ones, sample[...], preferred_element_type=F32)[:1]
    steps = jnp.round(total * TOTAL_STEPS).astype(jnp.int32)
    lines = [steps[:, at : at + block] for at in range(0, steps.shape[1], block)]
    fill = -(len(lines) + dosage.shape[0] + perm.shape[0]) % 16
    lines += [jnp.zeros((fill, block), jnp.int32)] if fill else []
    out_ref[...] = jnp.concatenate([dosage[...], perm[...], *lines], axis=0).astype(
        jnp.int16
    )


def join_kernel(first_rows, spare, mine_ref, theirs_ref, out_ref, held, sems):
    core = lax.rem(lax.axis_index("samp"), 2)
    fetches = [
        pltpu.make_async_copy(source, held.at[place], sems.at[place])
        for place, source in enumerate((mine_ref, theirs_ref))
    ]
    for fetch in fetches:
        fetch.start()
    for fetch in fetches:
        fetch.wait()
    mine, theirs = held[0], held[1]
    low = jnp.where(core == 0, mine, theirs)
    high = jnp.where(core == 0, theirs, mine)
    nulls = mine.shape[0] - first_rows
    at = first_rows
    out_ref[:at] = low[nulls:]
    out_ref[at : at + first_rows - spare] = high[nulls + spare :]
    at += first_rows - spare
    out_ref[at : at + nulls] = low[:nulls]
    out_ref[at + nulls :] = high[:nulls]


def place_ids(block):
    samp = lax.axis_index("samp")
    core = lax.rem(samp, 2)
    mate = samp + 1 - 2 * core
    groups = block // LANES
    ids = [samp * groups + group for group in range(groups)]
    ids += [mate * groups + group for group in range(groups)]
    return core, [value.astype(F32).astype(BF16) for value in ids]


def scatter(loaded, group_ids, snp_rows, nulls):
    dose = jnp.concatenate([value[:snp_rows] for value in loaded], axis=1)
    perm = jnp.concatenate([value[snp_rows : snp_rows + nulls] for value in loaded], axis=1)
    rows = snp_rows // PACK
    packed = dose[:rows]
    for part in range(1, PACK):
        packed = packed + dose[part * rows : (part + 1) * rows] * (4**part)
    packed = packed.astype(F32).astype(BF16)
    high = (perm // LANES).astype(F32).astype(BF16)
    low = (perm % LANES).astype(F32).astype(BF16)
    lane_ids = lax.broadcasted_iota(jnp.int32, (LANES, dose.shape[1]), 0)
    lane_ids = lane_ids.astype(F32).astype(BF16)
    one = jnp.ones((), BF16)
    zero = jnp.zeros((), BF16)
    for copy in range(nulls):
        onehot = jnp.where(lane_ids == low[copy : copy + 1], one, zero)
        masked = jnp.concatenate(
            [jnp.where(high[copy : copy + 1] == value, packed, zero) for value in group_ids],
            axis=0,
        )
        yield lax.dot_general(
            masked, onehot, (((1,), (1,)), ((), ())), preferred_element_type=F32
        )


def moments(loaded, snp_rows):
    dose = jnp.concatenate([value[:snp_rows] for value in loaded], axis=1).astype(F32)
    return (
        jnp.sum(dose, axis=1, keepdims=True),
        jnp.sum(dose * dose, axis=1, keepdims=True),
    )


def near_kernel(snp_rows, nulls, own_ref, mate_ref, weight_ref, *refs):
    spots_ref, first_ref, moment_ref, steps_ref, spread_weight_ref, held, sems = refs
    fetches = [
        pltpu.make_async_copy(small, held.at[place], sems.at[place])
        for place, small in enumerate((own_ref, mate_ref))
    ]
    for fetch in fetches:
        fetch.start()
    for fetch in fetches:
        fetch.wait()
    loaded = [held[place].astype(jnp.int32) for place in range(2)]
    block = loaded[0].shape[1]
    _, group_ids = place_ids(block)
    for copy, spots in enumerate(scatter(loaded, group_ids, snp_rows, nulls)):
        spots_ref[copy * spots.shape[0] : (copy + 1) * spots.shape[0], :] = spots
    for place, value in enumerate(loaded):
        first_ref[:, place * block : (place + 1) * block] = (
            value[:snp_rows].astype(F32).astype(BF16)
        )
    for place, value in enumerate(moments(loaded, snp_rows)):
        moment_ref[place * snp_rows : (place + 1) * snp_rows, :] = jnp.broadcast_to(
            value, (snp_rows, LANES)
        )
    at = snp_rows + nulls
    steps_ref[...] = (loaded[0] + loaded[1])[at : at + steps_ref.shape[0]]
    spot = lax.broadcasted_iota(jnp.int32, (snp_rows, snp_rows), 0)
    diagonal = spot == lax.broadcasted_iota(jnp.int32, (snp_rows, snp_rows), 1)
    weight = jnp.sum(jnp.where(diagonal, weight_ref[...], 0.0), axis=1, keepdims=True)
    spread_weight_ref[...] = jnp.broadcast_to(weight, spread_weight_ref.shape)


def score_kernel(copies, snp_rows, block, half, total_samples, *refs):
    smalls = refs[0:2]
    pheno_ref, mate_ref, spots_ref, own_ref, moment_ref, steps_ref = refs[2:8]
    chunks = len(CHUNK_LANES)
    chunk_refs = refs[8 : 8 + chunks]
    first_ref = refs[8 + chunks]
    picked, genes, held, near_spots, near_moments, near_steps, sems = refs[-7:]
    core, group_ids = place_ids(block)
    own_cols = pl.ds(pl.multiple_of(core * half, half), half)
    fetches = [
        pltpu.make_async_copy(
            source.at[:, own_cols], genes.at[pl.ds(place * block, block), :], sems.at[place]
        )
        for place, source in enumerate((pheno_ref, mate_ref))
    ]
    pairs = [(small, held.at[place]) for place, small in enumerate(smalls)]
    pairs += [
        (spots_ref, near_spots),
        (own_ref, picked.at[pl.ds(0, snp_rows), :]),
        (moment_ref, near_moments),
        (steps_ref, near_steps),
    ]
    fetches += [
        pltpu.make_async_copy(source, target, sems.at[2 + place])
        for place, (source, target) in enumerate(pairs)
    ]
    for fetch in fetches:
        fetch.start()
    for fetch in fetches[2:]:
        fetch.wait()
    nulls = copies - 1
    loaded = [held[place].astype(jnp.int32) for place in range(2)]
    at = snp_rows + nulls
    steps = (loaded[0] + loaded[1])[at : at + near_steps.shape[0]] + near_steps[...]
    lines = half // block
    center = jnp.concatenate(
        [
            jnp.where(core == 0, steps[line], steps[lines + line]).reshape(1, block)
            for line in range(lines)
        ],
        axis=1,
    ).astype(F32) * (CENTER_SHARE / (TOTAL_STEPS * total_samples))
    dose_sum, square_sum = moments(loaded, snp_rows)
    dose_mean = (dose_sum + near_moments[:snp_rows, :1]) / total_samples
    dose_square = (square_sum + near_moments[snp_rows:, :1]) / total_samples
    inv_spread = lax.rsqrt(total_samples * (dose_square + 1e-05))
    rows = snp_rows // PACK
    for copy, far_spots in enumerate(scatter(loaded, group_ids, snp_rows, nulls)):
        size = far_spots.shape[0]
        spots = (far_spots + near_spots[copy * size : (copy + 1) * size, :]).astype(jnp.int32)
        for group in range(size // rows):
            piece = spots[group * rows : (group + 1) * rows]
            for part in range(PACK):
                at = (copy + 1) * snp_rows + part * rows
                picked[at : at + rows, group * LANES : (group + 1) * LANES] = (
                    lax.shift_right_logical(piece, 2 * part) & 3
                ).astype(F32).astype(BF16)
    all_rows = copies * snp_rows
    picked[all_rows:, :] = jnp.ones((picked.shape[0] - all_rows, 2 * block), BF16)
    row_sum = jnp.sum(picked[:all_rows].astype(F32), axis=1, keepdims=True)
    mean_rows = jnp.concatenate([dose_mean] * copies, axis=0)
    inv_rows = jnp.concatenate([inv_spread] * copies, axis=0)
    excess = row_sum - mean_rows * (2.0 * block)
    for fetch in fetches[:2]:
        fetch.wait()
    raw = jnp.dot(picked[...], genes[...], preferred_element_type=F32)
    total = raw[all_rows : all_rows + 1]
    part = ((raw[:all_rows] - mean_rows * total - center * excess) * inv_rows).astype(BF16)
    first_ref[...] = part[:snp_rows]
    start = 0
    for chunk_ref in chunk_refs:
        stop = start + chunk_ref.shape[1]
        chunk_ref[...] = part[snp_rows:, start:stop]
        start = stop


def gram_kernel(pieces, *refs):
    chunks = len(CHUNK_LANES)
    inputs = refs[: 4 * chunks]
    weight_refs = refs[4 * chunks : 4 * chunks + 2]
    outs = refs[4 * chunks + 2 : -3]
    strip, held, sems = refs[-3:]
    rows = inputs[0].shape[0]
    copies = []
    for slab in range(2):
        start = 0
        for place in range(slab * 2 * chunks, (slab + 1) * 2 * chunks):
            source = inputs[place]
            copies.append(
                pltpu.make_async_copy(
                    source,
                    held.at[pl.ds(slab * rows, rows), pl.ds(start, source.shape[1])],
                    sems.at[place],
                )
            )
            copies[-1].start()
            start += source.shape[1]
    weight = jnp.concatenate(
        [
            weight_ref[:, :1]
            for weight_ref in weight_refs
            for _ in range(rows // weight_ref.shape[0])
        ],
        axis=0,
    )
    for copy in copies:
        copy.wait()
    samp = lax.axis_index("samp")
    snp = lax.axis_index("snp")
    width = held.shape[1] // BLOCKS
    first = ((samp // 2) * 2 + lax.rem(snp, 2)) * 2
    depth = snp // 2
    own = held[:, pl.ds(pl.multiple_of(first * width, width), 2 * width)].astype(F32)
    turned = (own * weight).T.astype(BF16)
    span = (REACH + 1) * width
    cover = held[:, pl.ds(pl.multiple_of(first * width, 2 * width), span)]
    image = jnp.dot(turned, cover, preferred_element_type=F32)
    for line in range(2):
        strip[line * width : (line + 1) * width, :] = image[
            line * width : (line + 1) * width, line * width : (line + REACH) * width
        ]
    size = 2 * width // pieces
    for step in range(pieces):
        at = lax.bitwise_xor(depth, step) * size
        outs[step][...] = strip[pl.ds(pl.multiple_of(at, size), size), :].astype(BF16)


def chain_kernel(pieces, total_rows, *refs):
    chunks = len(CHUNK_LANES)
    groups = GROUPS
    strips = refs[: 8 * groups]
    nulls = refs[8 * groups : 8 * groups + 2 * chunks]
    firsts = refs[8 * groups + 2 * chunks : 8 * groups + 2 * chunks + 2]
    own_ref, mate_ref, matrix, kept, current, sems = refs[8 * groups + 2 * chunks + 2 :]
    samp = lax.axis_index("samp")
    snp = lax.axis_index("snp")
    core = lax.rem(samp, 2)
    side = samp // 2
    minor = lax.rem(snp, 2)
    depth = snp // 2
    genes = matrix.shape[0]
    width = genes // BLOCKS
    size = 2 * width // pieces
    reach = REACH * width
    null_rows = nulls[0].shape[0] // 2
    first_rows = kept.shape[0] - null_rows
    for place, source in enumerate(strips):
        flips, group = divmod(place, groups)
        block = (
            flip_bit(core, flips // 4) * 8
            + flip_bit(side, flips // 2 % 2) * 4
            + flip_bit(minor, flips % 2) * 2
        )
        for inner in range(pieces // groups):
            piece = lax.bitwise_xor(depth, group * (pieces // groups) + inner)
            row = pl.multiple_of(block * width + piece * size, size)
            column = pl.multiple_of((row // width) * width, width)
            pltpu.make_async_copy(
                source.at[pl.ds(inner * size, size), :],
                matrix.at[pl.ds(row, size), pl.ds(column, reach)],
                sems.at[0],
            ).start()
    half = genes // 2
    for flip in range(2):
        holder = flip_bit(core, flip)
        start = 0
        for chunk in range(chunks):
            source = nulls[flip * chunks + chunk]
            column = pl.multiple_of(holder * half + start, LANES)
            pltpu.make_async_copy(
                source.at[pl.ds(pl.multiple_of(core * null_rows, null_rows), null_rows), :],
                kept.at[pl.ds(0, null_rows), pl.ds(column, source.shape[1])],
                sems.at[1],
            ).start()
            start += source.shape[1]
        skip = firsts[0].shape[0] - first_rows
        pltpu.make_async_copy(
            firsts[flip].at[pl.ds(pl.multiple_of(core * skip, 16), first_rows), :],
            kept.at[
                pl.ds(null_rows, first_rows), pl.ds(pl.multiple_of(holder * half, half), half)
            ],
            sems.at[1],
        ).start()
    filled = matrix.at[:, pl.ds(0, reach)]
    pltpu.make_async_copy(filled, filled, sems.at[0]).wait()
    pltpu.make_async_copy(kept, kept, sems.at[1]).wait()

    trace = jnp.zeros((1, 1), F32)
    eye = lax.broadcasted_iota(jnp.int32, (width, width), 0) == lax.broadcasted_iota(
        jnp.int32, (width, width), 1
    )
    diagonal = jnp.zeros((width, width), F32)
    for block in range(BLOCKS):
        at = slice(block * width, (block + 1) * width)
        diagonal = diagonal + jnp.where(eye, matrix[at, at].astype(F32), 0.0)
    trace = jnp.sum(jnp.sum(diagonal, axis=1, keepdims=True), axis=0, keepdims=True)
    scale = trace / total_rows / genes + 1e-06
    factor = 0.5 / (total_rows * scale)

    for block in range(BLOCKS):
        over = block + REACH - BLOCKS
        if over > 0:
            at = slice(block * width, (block + 1) * width)
            matrix[at, : over * width] = matrix[at, genes : genes + over * width]

    for block in range(BLOCKS):
        home = slice(block * width, (block + 1) * width)
        turned = matrix[home, (block + 1) * width : (block + REACH - 1) * width].T
        for step in range(1, REACH - 1):
            target = (block + step) % BLOCKS * width
            matrix[target : target + width, home] = turned[(step - 1) * width : step * width]

    def apply(source, target):
        image = jnp.dot(source[...], matrix[:, :genes], preferred_element_type=F32)
        target[...] = (1.5 * source[...].astype(F32) - factor * image).astype(BF16)

    first_image, second_image = current.at[0], current.at[1]
    apply(kept, first_image)
    apply(first_image, second_image)
    apply(second_image, kept)
    inverse = lax.rsqrt(scale)
    at = pl.ds(pl.multiple_of(side * half, half), half)
    image = jnp.dot(kept[...], matrix[:, at], preferred_element_type=F32)
    value = (1.5 * first_image[:, at].astype(F32) - factor * image) * inverse
    second_image[:, :half] = value.astype(BF16)
    quarter = half // 2
    for flip, out_ref in enumerate((own_ref, mate_ref)):
        base = pl.multiple_of(flip_bit(core, flip) * quarter, quarter)
        out_ref[...] = second_image[:, pl.ds(base, quarter)]


def shards(samp_count, snp_count, dosage, pheno, perm, snp_weight):
    snp_rows, block = dosage.shape
    genes = pheno.shape[1]
    total_samples = block * samp_count
    total_snps = snp_rows * snp_count
    null_count = perm.shape[0]
    copies = null_count + 1
    half = genes // 2
    width = genes // BLOCKS
    chunk_cols = [half * lanes // sum(CHUNK_LANES) for lanes in CHUNK_LANES]
    chunks = len(chunk_cols)
    null_rows = null_count * snp_rows
    pieces = snp_count // 2
    size = 2 * width // pieces
    groups = GROUPS

    def move(value, step):
        return permute(value, samp_count, snp_count, step)

    def over_core(value):
        return move(value, lambda a, b: (a ^ 1, b))

    def over_side(value):
        return move(value, lambda a, b: (a ^ 2, b))

    def over_both(value):
        return move(value, lambda a, b: (a ^ 3, b))

    def over_minor(value):
        return move(value, lambda a, b: (a, b ^ 1))

    def over_plane(value):
        return move(value, lambda a, b: (a ^ 2, b ^ 1))

    def over_depth(value, step):
        return move(value, lambda a, b: (a, b ^ (2 * step)))

    small_rows = snp_rows + null_count + genes // block
    small_rows += -small_rows % 16
    small = pl.pallas_call(
        pack_kernel,
        out_shape=jax.ShapeDtypeStruct((small_rows, block), jnp.int16),
        in_specs=[HBM] * 3,
        out_specs=VMEM,
        scratch_shapes=[
            pltpu.VMEM((block // CENTER_SHARE, genes), BF16),
            pltpu.VMEM(dosage.shape, jnp.int32),
            pltpu.VMEM(perm.shape, jnp.int32),
            pltpu.SemaphoreType.DMA((3,)),
        ],
        compiler_params=limit(60),
        name="pack",
    )(dosage, perm, pheno)
    smalls = [small, over_core(small), over_side(small), over_both(small)]
    mate_pheno = over_core(pheno)

    all_rows = copies * snp_rows
    shape = jax.ShapeDtypeStruct
    picks = 2 * block // LANES * (snp_rows // PACK)
    spots, near_first, moment, steps, weight = pl.pallas_call(
        functools.partial(near_kernel, snp_rows, null_count),
        out_shape=[
            shape((null_count * picks, LANES), F32),
            shape((snp_rows, 2 * block), BF16),
            shape((2 * snp_rows, LANES), F32),
            shape((genes // block, block), jnp.int32),
            shape((snp_rows, LANES), F32),
        ],
        in_specs=[ANY] * 2 + [VMEM],
        out_specs=[VMEM] * 5,
        scratch_shapes=[
            pltpu.VMEM((2, *small.shape), jnp.int16),
            pltpu.SemaphoreType.DMA((2,)),
        ],
        compiler_params=limit(16),
        name="near",
    )(smalls[0], smalls[1], snp_weight.reshape(1, snp_rows))
    parts = pl.pallas_call(
        functools.partial(score_kernel, copies, snp_rows, block, half, float(total_samples)),
        out_shape=[shape((null_rows, cols), BF16) for cols in chunk_cols]
        + [shape((snp_rows, half), BF16)],
        in_specs=[ANY] * 8,
        out_specs=[VMEM] * (chunks + 1),
        scratch_shapes=[
            pltpu.VMEM((all_rows + 16, 2 * block), BF16),
            pltpu.VMEM((2 * block, half), BF16),
            pltpu.VMEM((2, *small.shape), jnp.int16),
            pltpu.VMEM(spots.shape, F32),
            pltpu.VMEM(moment.shape, F32),
            pltpu.VMEM(steps.shape, jnp.int32),
            pltpu.SemaphoreType.DMA((8,)),
        ],
        compiler_params=limit(20),
        name="score",
    )(*smalls[2:], pheno, mate_pheno, spots, near_first, moment, steps)
    partial_first = parts[chunks]
    mate_weight = over_minor(weight)

    def finish(value):
        return (value.astype(F32) + over_side(value).astype(F32)).astype(BF16)

    own = [finish(value) for value in parts[:chunks]]
    own_first = finish(partial_first)
    mate = [over_core(value) for value in own]
    minor = [over_minor(value) for value in own]
    minor_mate = [over_core(value) for value in minor]
    mate_first = over_core(own_first)

    strips = pl.pallas_call(
        functools.partial(gram_kernel, pieces),
        out_shape=[shape((size, REACH * width), BF16)] * pieces,
        in_specs=[ANY] * (4 * chunks) + [VMEM] * 2,
        out_specs=[VMEM] * pieces,
        scratch_shapes=[
            pltpu.VMEM((2 * width, REACH * width), F32),
            pltpu.VMEM((2 * null_rows, genes), BF16),
            pltpu.SemaphoreType.DMA((4 * chunks,)),
        ],
        compiler_params=limit(20),
        name="gram",
    )(*own, *mate, *minor, *minor_mate, weight, mate_weight)

    piece = strips[0].astype(F32)
    for step in range(1, pieces):
        piece = piece + over_depth(strips[step], step).astype(F32)
    held = {0: piece.astype(BF16)}
    inner = pieces // groups
    bit = inner // 2
    while bit:
        for step in sorted(held):
            held[step + bit] = over_depth(held[step], bit)
        bit //= 2
    base = jnp.concatenate([held[step] for step in range(inner)], axis=0)
    plane = {}
    for far in (0, 2):
        near = far + 1
        at = over_depth(base, 2 * inner) if far else base
        plane[0, 0, far] = at
        plane[0, 0, near] = over_depth(at, inner)
        plane[1, 0, far] = over_side(at)
        plane[0, 1, far] = over_minor(at)
        plane[0, 1, near] = over_minor(plane[0, 0, near])
        plane[1, 0, near] = over_depth(plane[1, 0, far], inner)
        plane[1, 1, far] = over_side(plane[0, 1, far])
        plane[1, 1, near] = over_plane(plane[0, 0, near])
    places = [
        (side, minor, group) for side in range(2) for minor in range(2) for group in range(groups)
    ]
    plane_mate = [over_core(plane[place]) for place in places]
    plane = [plane[place] for place in places]

    first_rows = 32
    work_rows = null_rows // 2 + first_rows
    mine, other = pl.pallas_call(
        functools.partial(chain_kernel, pieces, float(null_count * total_snps)),
        out_shape=[shape((work_rows, genes // samp_count), BF16)] * 2,
        in_specs=[ANY] * (8 * groups + 2 * chunks + 2),
        out_specs=[VMEM] * 2,
        scratch_shapes=[
            pltpu.VMEM((genes, (BLOCKS + REACH - 1) * width), BF16),
            pltpu.VMEM((work_rows, genes), BF16),
            pltpu.VMEM((2, work_rows, genes), BF16),
            pltpu.SemaphoreType.DMA((2,)),
        ],
        compiler_params=limit(28),
        name="chain",
    )(*plane, *plane_mate, *own, *mate, own_first, mate_first)
    theirs = over_core(other)
    white = pl.pallas_call(
        functools.partial(join_kernel, first_rows, 2 * first_rows - snp_rows),
        out_shape=shape((all_rows, genes // samp_count), BF16),
        in_specs=[ANY] * 2,
        out_specs=VMEM,
        scratch_shapes=[
            pltpu.VMEM((2, *mine.shape), BF16),
            pltpu.SemaphoreType.DMA((2,)),
        ],
        compiler_params=limit(8),
        name="join",
    )(mine, theirs)
    return white.reshape(copies, snp_rows, genes // samp_count)


def layer(samp_count, snp_count, *args):
    return shards(samp_count, snp_count, *args)


def solution(mesh):
    samp_count, snp_count = mesh.shape["samp"], mesh.shape["snp"]
    return jax.shard_map(
        functools.partial(layer, samp_count, snp_count),
        mesh=mesh,
        in_specs=(P("snp", "samp"), P("samp", None), P(None, "samp"), P("snp")),
        out_specs=P(None, "snp", "samp"),
        check_vma=False,
    )
```
